32 devices in a mesh: section: 2 (over x), head: 4 (over y, core), tok: 4 (over z).
Axes of the slice: x: 2, y: 2, z: 4, core: 2. Of those that a mesh axis runs over, the one named last changes fastest.
Arguments:
- held_cotangents: bfloat16 [2, 2, 512, 2560], P('section', None, 'tok', 'head'), may hold values from -6 to 6
- entering_adjoint: bfloat16 [512, 2560], P('tok', 'head'), may hold values from -6 to 6
- saved_queries: bfloat16 [2, 512, 2560], P('section', 'tok', 'head'), may hold values from -1024 to 1024
- saved_keys: bfloat16 [2, 512, 2560], P('section', 'tok', 'head'), may hold values from -20 to 20
- value_weight: bfloat16 [2, 2560, 2560], P('section', None, 'head'), may hold values from -0.125 to 0.125
- out_weight: bfloat16 [2, 2560, 2560], P('section', 'tok', 'head'), may hold values from -0.125 to 0.125
- block_gate: float32 [2, 2560], P('section'), may hold values from -3 to 3
- time_gate: float32 [32, 2560], replicated, may hold values from -3 to 3
- timestep: int32 [1], replicated, may hold values from 0 to 31
Outputs:
- passed: bfloat16 [2, 2, 512, 2560], P('section', None, 'tok', 'head')
The draws below stay inside these ranges and needn't reach their ends.
All inputs are finite; a program needn't handle non-finite values.
Results may differ from the reference program's by a relative error of at most 0.0085.
Values may be sent and summed in bfloat16 or wider, within the bound.
No kernel may reach another device: no remote copies, remote signals or barrier semaphores. Data moves between devices by JAX's collectives and lax.ppermute only.
A program may use at most 64 MiB of HBM per device.

```python
import jax
import jax.numpy as jnp
from jax import lax

D = 2560
HEADS = 20
HD = 128
NSTEPS = 32
TOK_SH = 128
SECTIONS = 2
TOKENS = 512
N_HEAD = 4
N_TOK = 4


def paired_rows(key):
    full_shape = (SECTIONS, TOKENS, HEADS, HD)
    query_vals = 1.6 * jax.random.truncated_normal(jax.random.fold_in(key, 101), -4.0, 4.0, full_shape)
    key_vals = 1.6 * jax.random.truncated_normal(jax.random.fold_in(key, 102), -4.0, 4.0, full_shape)
    return (query_vals.reshape(SECTIONS, TOKENS, HEADS * HD), key_vals.reshape(SECTIONS, TOKENS, HEADS * HD))


def draw_saved_queries(key, part):
    return paired_rows(key)[0].astype(jnp.bfloat16)


def draw_saved_keys(key, part):
    return paired_rows(key)[1].astype(jnp.bfloat16)


def block_scale(key, extent, split, low, high):
    level, own = 1.0, jax.random.fold_in(key, 6)
    for position, shards_of in split:
        draws = jnp.exp(jax.random.uniform(jax.random.fold_in(own, position), (shards_of,), jnp.float32, low / len(split), high / len(split)))
        level = level * jnp.repeat(draws, extent[position] // shards_of).reshape([-1 if axis == position else 1 for axis in range(len(extent))])
    return level


def gaussian(stream_key, dims, deviation, bound, shards=(), held_as=jnp.bfloat16):
    level = block_scale(stream_key, dims, shards, -0.22, 0.18) if shards else 1.0
    result = jax.random.normal(stream_key, dims, jnp.float32) * deviation * level
    return jnp.minimum(jnp.maximum(result, -bound), bound).astype(held_as)


def setup_inputs(seed: int = 0) -> dict:
    splits = jax.random.split(jax.random.key(seed), 10)
    held_cotangents = gaussian(splits[0], (SECTIONS, 2, TOKENS, D), 1.0, 6.0, ((0, 2), (2, 4), (3, 4)))
    entering_adjoint = gaussian(splits[1], (TOKENS, D), 1.0, 6.0, ((0, 4), (1, 4)))
    saved_queries = draw_saved_queries(jax.random.fold_in(splits[9], 71), 0)
    saved_keys = draw_saved_keys(jax.random.fold_in(splits[9], 71), 0)
    value_weight = gaussian(splits[4], (SECTIONS, D, HEADS * HD), D ** -0.5, 0.125, ((0, 2), (2, 4)))
    out_weight = gaussian(splits[5], (SECTIONS, D, HEADS * HD), (HEADS * HD) ** -0.5, 0.125, ((0, 2), (1, 4), (2, 4)))
    block_gate = gaussian(splits[6], (SECTIONS, D), 0.6, 3.0, ((0, 2),), jnp.float32)
    time_gate = gaussian(splits[7], (NSTEPS, D), 0.6, 3.0, (), jnp.float32)
    timestep = jax.random.randint(splits[8], (1,), 0, NSTEPS).astype(jnp.int32)
    return {"held_cotangents": held_cotangents, "entering_adjoint": entering_adjoint, "saved_queries": saved_queries, "saved_keys": saved_keys, "value_weight": value_weight, "out_weight": out_weight, "block_gate": block_gate, "time_gate": time_gate, "timestep": timestep}


GUIDE = 3.0

def section_vjp(inputs):
    held_section, query_section, key_section, value_section, output_section, gate_row = inputs
    rows_all = held_section.shape[1]
    width = held_section.shape[2]
    scaled = (held_section.astype(jnp.float32) * gate_row).astype(jnp.bfloat16)
    attn_grad = jnp.dot(scaled.reshape(2 * rows_all, width), output_section, preferred_element_type=jnp.float32)
    attn_grad = attn_grad.astype(jnp.bfloat16).reshape(2, rows_all, HEADS * HD)
    query_heads = jnp.transpose(query_section.reshape(rows_all, HEADS, HD), (1, 0, 2))
    key_heads = jnp.transpose(key_section.reshape(rows_all, HEADS, HD), (1, 0, 2))
    grad_heads = jnp.transpose(attn_grad[0].reshape(rows_all, HEADS, HD), (1, 0, 2))

    def one_head(head_inputs):
        query_one, key_one, grad_one = head_inputs
        scores = jnp.dot(query_one, key_one.T, preferred_element_type=jnp.float32) * HD ** (-0.5)
        row_top = lax.optimization_barrier(jnp.max(scores, axis=1, keepdims=True))
        log_total = row_top + jnp.log(lax.optimization_barrier(jnp.sum(jnp.exp(scores - row_top), axis=1, keepdims=True)))
        weights = jnp.exp(scores - log_total).astype(jnp.bfloat16)
        blocked = jnp.einsum('bij,bie->bje', weights.reshape(N_TOK, TOK_SH, rows_all).astype(jnp.float32), grad_one.reshape(N_TOK, TOK_SH, HD).astype(jnp.float32), precision=lax.Precision.HIGHEST)
        blocked = lax.optimization_barrier(blocked.astype(jnp.bfloat16))
        return lax.optimization_barrier(jnp.sum(blocked.astype(jnp.float32), axis=0)).astype(jnp.bfloat16)
    normal_value = lax.map(one_head, (query_heads, key_heads, grad_heads))
    normal_value = jnp.transpose(normal_value, (1, 0, 2)).reshape(rows_all, HEADS * HD)
    value_grad = jnp.stack([normal_value, attn_grad[1]])
    group_width = HEADS * HD // N_HEAD
    back_sum = jnp.zeros((2 * rows_all, width), jnp.float32)
    for group_index in range(N_HEAD):
        lower = group_index * group_width
        upper_col = lower + group_width
        partial_value = jnp.dot(value_grad[:, :, lower:upper_col].reshape(2 * rows_all, group_width), value_section[:, lower:upper_col].T, preferred_element_type=jnp.float32)
        partial_value = lax.optimization_barrier(partial_value.astype(jnp.bfloat16))
        back_sum = back_sum + partial_value.astype(jnp.float32)
    return (held_section.astype(jnp.float32) + back_sum.reshape(2, rows_all, width)).astype(jnp.bfloat16)

def reference(held_cotangents, entering_adjoint, saved_queries, saved_keys, value_weight, out_weight, block_gate, time_gate, timestep):
    step_ids = jnp.arange(NSTEPS).astype(jnp.int32)
    time_row = lax.optimization_barrier(jnp.sum(jnp.where((step_ids == timestep[0])[:, None], time_gate, jnp.zeros_like(time_gate)), axis=0))
    gates = block_gate + time_row[None, :]
    block_cots = lax.map(section_vjp, (held_cotangents, saved_queries, saved_keys, value_weight, out_weight, gates))
    entering_full = entering_adjoint.astype(jnp.float32)
    fresh_rows = jnp.stack([(1.0 + GUIDE) * entering_full, -GUIDE * entering_full]).astype(jnp.bfloat16)
    return jnp.concatenate([block_cots[1:], fresh_rows[None]], axis=0)
```

```python
import functools

import jax
import jax.numpy as jnp
from jax import lax
from jax.experimental import pallas as pl
from jax.experimental.pallas import tpu as pltpu
from jax.sharding import PartitionSpec as P

HD = 128


GUIDE = 3.0


AXES = ("section", "head", "tok")
ORDER = (0, 2, 1, 3)


def combined_all(part, axis, combine):
    gathered = jax.tree.map(lambda a: lax.all_gather(a, axis), part)

    def take(source):
        return jax.tree.map(lambda a: lax.dynamic_index_in_dim(a, source, 0, False), gathered)

    return lax.fori_loop(
        1, lax.axis_size(axis), lambda source, state: combine(state, take(source)), take(0)
    )


def shifted(value, axis, steps):
    count = lax.axis_size(axis)
    leading, last = (max(0, -steps), min(count, count - steps))
    return lax.ppermute(value, axis, [(source, source + steps) for source in range(leading, last)])


def merge_stats(earlier, latter):
    row_top = jnp.maximum(earlier[0], latter[0])
    total_sum = earlier[1] * jnp.exp(earlier[0] - row_top) + latter[1] * jnp.exp(
        latter[0] - row_top
    )
    return (row_top, total_sum)


def fresh_of(entering_adjoint):
    entering_full = entering_adjoint.astype(jnp.float32)
    return jnp.stack([(1.0 + GUIDE) * entering_full, -GUIDE * entering_full]).astype(jnp.bfloat16)


def general_body(
    held_cotangents,
    entering_adjoint,
    saved_queries,
    saved_keys,
    value_weight,
    out_weight,
    block_gate,
    time_gate,
    timestep,
):
    steps_index = jnp.arange(time_gate.shape[0])
    time_row = jnp.sum(
        jnp.where((steps_index == timestep[0])[:, None], time_gate, jnp.zeros_like(time_gate)),
        axis=0,
    )
    gate_row = block_gate[0] + time_row
    whole_cot = lax.all_gather(held_cotangents[0], "head", axis=2, tiled=True)
    scaled = (whole_cot.astype(jnp.float32) * gate_row).astype(jnp.bfloat16)
    out_full = lax.all_gather(out_weight[0], "tok", axis=0, tiled=True)
    attn_grad = jnp.einsum(
        "btd,dk->btk", scaled, out_full, preferred_element_type=jnp.float32
    ).astype(jnp.bfloat16)
    rows_here = saved_queries.shape[1]
    groups_here = saved_queries.shape[2] // HD
    score_scale = HD ** (-0.5)
    normal_grad = attn_grad[0]
    query_all = lax.all_gather(saved_queries[0], "tok", axis=0, tiled=True)
    total_rows = query_all.shape[0]
    shards = total_rows // rows_here
    key_heads = saved_keys[0].reshape(rows_here, groups_here, HD)
    scores = (
        jnp.einsum(
            "ihe,jhe->hij",
            query_all.reshape(total_rows, groups_here, HD),
            key_heads,
            preferred_element_type=jnp.float32,
        )
        * score_scale
    )
    row_top = jnp.max(scores, axis=2)
    partial_total = jnp.sum(jnp.exp(scores - row_top[:, :, None]), axis=2)
    top_all, total_all = combined_all((row_top, partial_total), "tok", merge_stats)
    log_total = top_all + jnp.log(total_all)
    weights = jnp.exp(scores - log_total[:, :, None]).astype(jnp.bfloat16)
    grad_all = lax.all_gather(normal_grad, "tok", axis=0, tiled=True)
    blocked = jnp.einsum(
        "hbij,bihe->bjhe",
        weights.reshape(groups_here, shards, rows_here, rows_here),
        grad_all.reshape(shards, rows_here, groups_here, HD),
        preferred_element_type=jnp.float32,
    )
    blocked = lax.optimization_barrier(blocked.astype(jnp.bfloat16))
    value_grad = (
        jnp.sum(blocked.astype(jnp.float32), axis=0)
        .reshape(rows_here, groups_here * HD)
        .astype(jnp.bfloat16)
    )
    stacked = jnp.stack([value_grad, attn_grad[1]])
    partial_back = jnp.einsum(
        "btk,dk->btd", stacked, value_weight[0], preferred_element_type=jnp.float32
    )
    back_sum = lax.psum_scatter(
        partial_back.astype(jnp.bfloat16), "head", scatter_dimension=2, tiled=True
    ).astype(jnp.float32)
    block_cot = (held_cotangents[0].astype(jnp.float32) + back_sum).astype(jnp.bfloat16)
    passed_on = shifted(block_cot, "section", -1)
    is_last = lax.axis_index("section") == lax.axis_size("section") - 1
    return jnp.where(is_last, fresh_of(entering_adjoint), passed_on)[None]


def scale_kernel(ids, held, block_gate, time_rows, first, second):
    row = lax.rem(ids[0], time_rows.shape[0])
    gate = block_gate[...] + time_rows[pl.ds(row, 1), :]
    first[...] = (held[0].astype(jnp.float32) * gate).astype(first.dtype)
    second[...] = (held[1].astype(jnp.float32) * gate).astype(second.dtype)


def scale(held, block_gate, time_gate, timestep, head):
    _, rows, width = held.shape
    steps = time_gate.shape[0]
    step_rows = 8 if steps % 8 == 0 else steps
    ids = jnp.stack([timestep[0], head]).astype(jnp.int32)
    shape = jax.ShapeDtypeStruct((rows, width), held.dtype)
    return pl.pallas_call(
        scale_kernel,
        out_shape=(shape, shape),
        grid_spec=pltpu.PrefetchScalarGridSpec(
            num_scalar_prefetch=1,
            grid=(1,),
            in_specs=[
                pl.BlockSpec((2, rows, width), lambda i, ids: (0, 0, 0)),
                pl.BlockSpec((1, width), lambda i, ids: (0, ids[1])),
                pl.BlockSpec((step_rows, width), lambda i, ids: (ids[0] // step_rows, ids[1])),
            ],
            out_specs=[pl.BlockSpec((rows, width), lambda i, ids: (0, 0))] * 2,
        ),
        name="scale",
    )(ids, held, block_gate, time_gate)


def weights_kernel(*refs):
    *blocks, out = refs
    queries = jnp.concatenate([b[0] for b in blocks], axis=0)
    keys = jnp.concatenate([b[1] for b in blocks], axis=0)
    scores = (
        lax.dot_general(
            keys, queries, (((1,), (1,)), ((), ())), preferred_element_type=jnp.float32
        )
        * HD ** (-0.5)
    )
    raised = jnp.exp(scores - jnp.max(scores, axis=0, keepdims=True))
    total = jnp.sum(raised, axis=0, keepdims=True)
    out[0] = (raised * (1.0 / total)).astype(out.dtype)


def attention_weights(blocks):
    _, rows, width = blocks[0].shape
    heads = width // HD
    total = rows * len(blocks)
    return pl.pallas_call(
        weights_kernel,
        out_shape=jax.ShapeDtypeStruct((heads, total, total), jnp.bfloat16),
        grid=(heads,),
        in_specs=[pl.BlockSpec((2, rows, HD), lambda h: (0, 0, h))] * len(blocks),
        out_specs=pl.BlockSpec((1, total, total), lambda h: (h, 0, 0)),
        cost_estimate=pl.CostEstimate(
            flops=2 * heads * total * total * HD,
            transcendentals=heads * total * total,
            bytes_accessed=4 * heads * total * total,
        ),
        name="attention_weights",
    )(*blocks)


def product_kernel(flags, b0, b1, b2, b3, sibling, own_weight, sent_weight, weights, keep, send, x):
    rows = b0.shape[0]
    half = keep.shape[0]

    @pl.when(flags[1] == 1)
    def _():
        for i, b in enumerate((b0, b1, b2, b3)):
            x[pl.ds(i * rows, rows), :] = b[...]

    @pl.when(flags[1] == 0)
    def _():
        for i in range(4):
            x[pl.ds(i * rows, rows), :] = sibling[i]

    @pl.when(flags[0] == 1)
    def _():
        grad = jnp.dot(x[...], own_weight[...], preferred_element_type=jnp.float32)
        grad = grad.astype(keep.dtype)
        for h in range(weights.shape[0]):
            cols = slice(h * HD, (h + 1) * HD)
            mixed = jnp.dot(weights[h], grad[:, cols], preferred_element_type=jnp.float32)
            mixed = mixed.astype(keep.dtype)
            keep[:, cols] = mixed[:half]
            send[:, cols] = mixed[half:]

    @pl.when(flags[0] == 0)
    def _():
        grad = jnp.dot(x[...], sent_weight[...], preferred_element_type=jnp.float32)
        grad = grad.astype(keep.dtype)
        keep[...] = grad[:half]
        send[...] = grad[half:]


def product(flags, blocks, sibling, own_weight, sent_weight, weights):
    rows, width = blocks[0].shape
    cols = own_weight.shape[1]
    shape = jax.ShapeDtypeStruct((2 * rows, cols), jnp.bfloat16)
    vmem = pl.BlockSpec(memory_space=pltpu.VMEM)
    return pl.pallas_call(
        product_kernel,
        out_shape=(shape, shape),
        in_specs=[pl.BlockSpec(memory_space=pltpu.SMEM)] + [vmem] * 8,
        out_specs=[vmem] * 2,
        scratch_shapes=[pltpu.VMEM((4 * rows, width), jnp.bfloat16)],
        cost_estimate=pl.CostEstimate(
            flops=2 * 4 * rows * cols * (width + 4 * rows),
            transcendentals=0,
            bytes_accessed=8 * rows * cols * 4,
        ),
        name="product",
    )(flags, *blocks, sibling, own_weight, sent_weight, weights)


def back_kernel(head, value, weight, keep, send):
    slice_rows = keep.shape[2]
    for out, which in ((keep, (0, 2)), (send, (1, 3))):
        for i, k in enumerate(which):
            start = pl.multiple_of((head[0] ^ k) * slice_rows, 128)
            out[i] = lax.dot_general(
                value[...],
                weight[pl.ds(start, slice_rows), :],
                (((1,), (1,)), ((), ())),
                preferred_element_type=jnp.float32,
            ).astype(out.dtype)


def back_product(head, value, weight):
    rows, cols = value.shape
    depth = weight.shape[0]
    slice_rows = depth // 4
    shape = jax.ShapeDtypeStruct((2, rows, slice_rows), jnp.bfloat16)
    vmem = pl.BlockSpec(memory_space=pltpu.VMEM)
    return pl.pallas_call(
        back_kernel,
        out_shape=(shape, shape),
        in_specs=[pl.BlockSpec(memory_space=pltpu.SMEM), vmem, vmem],
        out_specs=[vmem] * 2,
        cost_estimate=pl.CostEstimate(
            flops=2 * rows * cols * depth, transcendentals=0, bytes_accessed=2 * depth * cols
        ),
        name="back_product",
    )(head, value, weight)


def added(*parts):
    total = parts[0].astype(jnp.float32)
    for part in parts[1:]:
        total = total + part.astype(jnp.float32)
    return total.astype(jnp.bfloat16)


def folded_body(
    held_cotangents,
    entering_adjoint,
    saved_queries,
    saved_keys,
    value_weight,
    out_weight,
    block_gate,
    time_gate,
    timestep,
):
    sections, heads, toks = (lax.axis_size(a) for a in AXES)
    section, head, tok = (lax.axis_index(a) for a in AXES)
    first, last = 0, sections - 1

    def move(value, target, only=None):
        pairs = []
        for s in range(sections):
            for h in range(heads):
                for t in range(toks):
                    if only is not None and not only(s, h, t):
                        continue
                    to = target(s, h, t)
                    pairs.append(
                        tuple((a * heads + b) * toks + c for a, b, c in ((s, h, t), to))
                    )
        return lax.ppermute(value, AXES, pairs)

    def along_tok(k):
        return lambda s, h, t: (s, h, t ^ k)

    def along_head(k):
        return lambda s, h, t: (s, h ^ k, t)

    working = section == last
    up = lambda s, h, t: (last, h, t)
    down = lambda s, h, t: (first, h, t)
    is_last = lambda s, h, t: s == last
    is_first = lambda s, h, t: s == first

    held = held_cotangents[0]
    pair0 = jnp.stack([saved_queries[0], saved_keys[0]])
    pair2 = move(pair0, along_tok(2), is_last)
    pair1 = move(pair0, along_tok(1), is_last)
    pair3 = move(pair2, along_tok(1), is_last)

    normal, identity = scale(held, block_gate, time_gate, timestep, head)
    identity = move(identity, down, is_last)
    sent_weight = move(out_weight[0], down, is_last)
    mine = jnp.where(working, normal, identity)

    other = move(mine, along_head(2))
    home = (tok >> 1) == (head >> 1)
    near = jnp.where(home, mine, other)
    far = jnp.where(home, other, mine)
    receives = lambda s, h, t: (t & 1) == (h & 1)
    gives = lambda s, h, t: (t & 1) != (h & 1)
    got1 = move(near, along_tok(1), gives)
    got2 = move(far, along_tok(2), receives)
    got3 = move(far, along_tok(3), gives)
    blocks = (near, got2, got1, got3)
    sibling = move(jnp.stack(blocks), along_head(1), receives)

    weights = attention_weights((pair0, pair2, pair1, pair3))
    flags = jnp.stack([working, (tok & 1) == (head & 1)]).astype(jnp.int32)
    keep, send = product(flags, blocks, sibling, out_weight[0], sent_weight, weights)

    rows = held.shape[1]
    arrived = move(send, along_tok(1))
    passing = added(keep[rows:], arrived[rows:])
    arrived2 = move(passing, along_tok(2))
    value0 = added(keep[:rows], arrived[:rows], arrived2)
    value1 = move(value0, up, is_first)

    head_id = head.reshape(1).astype(jnp.int32)
    outs = []
    for branch, value in enumerate((value0, value1)):
        keep, send = back_product(head_id, value, value_weight[0])
        arrived = move(send, along_head(1), is_last)
        passing = added(keep[1], arrived[1])
        arrived2 = move(passing, along_head(2), is_last)
        block_cot = added(held[branch], added(keep[0], arrived[0], arrived2))
        outs.append(move(block_cot, down, is_last))
    passed_on = jnp.stack(outs)
    return jnp.where(working, fresh_of(entering_adjoint), passed_on)[None]


def solution(mesh):
    shape = mesh.shape
    folds = shape["section"] == 2 and shape["head"] == 4 and shape["tok"] == 4
    return jax.shard_map(
        folded_body if folds else general_body,
        mesh=mesh,
        in_specs=(
            P("section", None, "tok", "head"),
            P("tok", "head"),
            P("section", "tok", "head"),
            P("section", "tok", "head"),
            P("section", None, "head"),
            P("section", "tok", "head"),
            P("section", None),
            P(),
            P(),
        ),
        out_specs=P("section", None, "tok", "head"),
        check_vma=False,
    )
```
